128 devices in a mesh: walk: 2 (over core), orb: 64 (over z, y, x).
Axes of the slice: x: 4, y: 4, z: 4, core: 2. Of those that a mesh axis runs over, the one named last changes fastest.
Arguments:
- inverse: float32 [8, 2048, 2048], P('walk', 'orb'), may hold values from -6 to 6
- table: bfloat16 [512, 64, 2048], P(None, None, 'orb'), may hold values from -0.0119018555 to 0.0119018555
- old_rows: float32 [8, 16, 2048], P('walk', None, 'orb'), may hold values from -0.0046403883 to 0.0046403883
- spline_weights: bfloat16 [8, 16, 64], P('walk'), may hold values from 0.0099487305 to 0.099609375
- tile_index: int32 [8, 16], P('walk'), may hold values from 0 to 511
- electrons: int32 [8, 16], P('walk'), may hold values from 0 to 2047, as said below
- accepts: int32 [8, 16], P('walk'), may hold values 0 or 1
- offspring: int32 [8], P('walk'), may hold values from 0 to 3, as said below
Outputs:
- ratios: float32 [8, 16], P('walk')
- new_inverse: float32 [8, 2048, 2048], P('walk', 'orb')
The draws below stay inside these ranges and needn't reach their ends.
Inputs may be any that keep to these rules, and one draw needn't show every extreme that they name: The 16 electrons of one walker are distinct. `offspring`: the counts of all walkers sum to 8.
All inputs are finite; a program needn't handle non-finite values. No bound on the sum of `accepts` on one device may be relied on, other than what follows from the above.
Results may differ from the reference program's by a relative error of at most 0.0003.
Values sent between devices are 32-bit elements; how exact they have to be, the bound alone decides.
A program may use at most 64 MiB of HBM per device.

```python
import math
import jax
import jax.numpy as jnp
from jax import lax

ORBS = 2048
K = 16
COEF = 64
TILES = 512
WALKERS = 8


def draw_electrons(key, part):
    keys = jax.random.split(key, WALKERS)
    rows = jax.vmap(lambda single: jax.random.permutation(single, ORBS)[:K])(keys)
    inner = 1 + jax.random.permutation(jax.random.fold_in(key, 7), ORBS - 2)[:K - 2]
    first = jnp.concatenate([jnp.array([0, ORBS - 1], dtype=jnp.int32), inner.astype(jnp.int32)])
    return rows.astype(jnp.int32).at[0].set(first)


def draw_offspring(key, part):
    ranks = jax.random.permutation(key, WALKERS)
    quarter = WALKERS // 4
    counts = jnp.where(ranks < quarter, 0, jnp.where(ranks < 2 * quarter, 2, 1))
    counts = jnp.where(ranks == quarter, 3, counts)
    counts = jnp.where(ranks == 2 * quarter, 0, counts)
    return counts.astype(jnp.int32)


def place_ends(values, rng, low, top_value):
    spot = [jax.random.randint(jax.random.fold_in(rng, axis), (), 0, length) for axis, length in enumerate(values.shape)]
    longest = values.shape.index(max(values.shape))
    beside = spot[:longest] + [(spot[longest] + 1) % values.shape[longest]] + spot[longest + 1:]
    return values.at[tuple(spot)].set(low).at[tuple(beside)].set(top_value)


def block_levels(stream_key, shape, cuts, smallest, high):
    level, own = 1.0, jax.random.fold_in(stream_key, 6)
    for position, shards_of in cuts:
        heights = jnp.exp(jax.random.uniform(jax.random.fold_in(own, position), (shards_of,), jnp.float32, smallest / len(cuts), high / len(cuts)))
        level = level * jnp.repeat(heights, shape[position] // shards_of).reshape([-1 if axis == position else 1 for axis in range(len(shape))])
    return level


def centred(own_key, extent, deviation, most, pieces=(), held_as=jnp.bfloat16):
    entries = deviation * jax.random.normal(own_key, extent, jnp.float32)
    if pieces:
        entries = entries * block_levels(own_key, extent, pieces, -0.22, 0.18)
    return jnp.clip(entries, -most, most).astype(held_as)


def setup_inputs(seed: int = 0) -> dict:
    arg_keys = jax.random.split(jax.random.key(seed), 9)
    inverse = centred(arg_keys[0], (WALKERS, ORBS, ORBS), 1.0, 6.0, ((0, 2), (1, 64)), jnp.float32)
    table = centred(arg_keys[1], (TILES, COEF, ORBS), (0.09 / ORBS ** 0.5), 0.0119018555, ((2, 64),))
    old_rows = centred(arg_keys[2], (WALKERS, K, ORBS), (0.035 / ORBS ** 0.5), 0.0046403883, ((0, 2), (2, 64)), jnp.float32)
    spline_weights = jnp.clip(jnp.exp(math.log(0.099609375) - 2.3038113 * jax.random.uniform(arg_keys[3], (WALKERS, K, COEF), jnp.float32) ** block_levels(arg_keys[3], (WALKERS, K, COEF), ((0, 2),), -0.2, 0.2)), 0.0099487305, 0.099609375).astype(jnp.bfloat16)
    tile_index = place_ends(jax.random.randint(arg_keys[4], (WALKERS, K), 0, TILES), jax.random.fold_in(arg_keys[4], 1), 0, TILES - 1).astype(jnp.int32)
    electrons = draw_electrons(jax.random.fold_in(arg_keys[8], 71), 0)
    accepts = place_ends((jax.random.randint(arg_keys[6], (WALKERS, K), 0, 4) < 3).astype(jnp.int32), jax.random.fold_in(arg_keys[6], 1), 0, 1)
    offspring = draw_offspring(jax.random.fold_in(arg_keys[8], 71), 0)
    return dict(inverse=inverse, table=table, old_rows=old_rows, spline_weights=spline_weights, tile_index=tile_index, electrons=electrons, accepts=accepts, offspring=offspring)


def solve_small(matrix, rhs):
    count = matrix.shape[0]
    for index in range(count):
        pivot = matrix[index, index]
        mrow = matrix[index] / pivot
        brow = rhs[index] / pivot
        factor = matrix[:, index].at[index].set(0.0)
        matrix = matrix - factor[:, None] * mrow[None, :]
        matrix = matrix.at[index].set(mrow)
        rhs = rhs - factor[:, None] * brow[None, :]
        rhs = rhs.at[index].set(brow)
    return rhs


def move_ratios(cross, accept):
    count = cross.shape[0]
    order = jnp.arange(count)
    eye = jnp.eye(count, dtype=jnp.float32)

    def single(step):
        mask = accept * (order < step).astype(jnp.float32)
        system = eye + mask[:, None] * cross
        column = jnp.take(cross, step, axis=1)
        solved = solve_small(system, (mask * column)[:, None])[:, 0]
        rowm = jnp.take(cross, step, axis=0)
        return 1.0 + jnp.take(column, step) - jnp.sum(rowm * solved)

    return jax.vmap(single)(order)


def finish(inverse_one, projected, elec, accept):
    count = elec.shape[0]
    cross = projected[:, elec]
    system = jnp.eye(count, dtype=jnp.float32) + accept[:, None] * cross
    right = solve_small(system, accept[:, None] * projected)
    left = inverse_one[:, elec]
    return inverse_one - jnp.dot(left, right, precision=lax.Precision.HIGHEST), cross


def reference(inverse, table, old_rows, spline_weights, tile_index, electrons, accepts, offspring):
    def walker(args):
        inverse_one, olds, weights, tiles, elec, acc = args
        picked = table[tiles].astype(jnp.float32)
        rows = jnp.einsum("kc,kco->ko", weights.astype(jnp.float32), picked)
        change = rows - olds
        projected = jnp.dot(change, inverse_one, precision=lax.Precision.HIGHEST)
        accept = acc.astype(jnp.float32)
        updated, cross = finish(inverse_one, projected, elec, accept)
        return updated, move_ratios(cross, accept)

    updated, ratios = lax.map(walker, (inverse, old_rows, spline_weights, tile_index, electrons, accepts))
    ends = jnp.cumsum(offspring)
    slots = jnp.arange(offspring.shape[0]).astype(jnp.int32)
    source = jnp.sum((ends[None, :] <= slots[:, None]).astype(jnp.int32), axis=1).astype(jnp.int32)
    return ratios, jnp.take(updated, source, axis=0)
```

```python
import functools

import jax
import jax.numpy as jnp
from jax import lax
from jax.experimental import pallas as pl
from jax.experimental.pallas import tpu as pltpu
from jax.sharding import PartitionSpec as P

MESH = pl.DeviceIdType.MESH
HI = lax.Precision.HIGHEST
OWN = 4
OTHER = 3
K = 16
BLOCKS = 16


def shifted(me, step, n, sign):
    if n == 64:
        out = 0
        for scale in (16, 4, 1):
            digit = lax.rem(lax.div(me, scale), 4)
            move = lax.rem(lax.div(step, scale), 4)
            out = out + scale * lax.rem(digit + sign * move + 4, 4)
        return out
    return lax.rem(me + sign * step + n, n)


def exchange(
    n,
    inv_hbm, table_hbm, old_ref, wts_ref, tile_ref, elec_ref, acc_ref, off_ref,
    rows_out, inv_out, elec_out, acc_out, off_out,
    table, term, parts, tiles,
    load_sem, inv_send, inv_recv, int_send, int_recv,
    rs_send, rs_recv, ag_send, ag_recv, fw_send, fw_recv,
):
    me = lax.axis_index("orb")
    core = lax.axis_index("walk")
    partner = {"walk": 1 - core}
    share = OWN * BLOCKS // n
    first = 1 - core

    barrier = pltpu.get_barrier_semaphore()

    load_inv = pltpu.make_async_copy(inv_hbm, inv_out.at[pl.ds(0, OWN)], load_sem.at[0])
    load_table = pltpu.make_async_copy(table_hbm, table, load_sem.at[1])
    load_table.start()
    load_inv.start()

    pl.semaphore_signal(barrier, inc=1, device_id=partner, device_id_type=MESH)

    def greet(step, carry):
        pl.semaphore_signal(
            barrier, inc=1, device_id={"orb": shifted(me, step, n, 1)}, device_id_type=MESH
        )
        return carry

    lax.fori_loop(1, n, greet, 0)

    elec_out[0] = elec_ref[...]
    acc_out[0] = acc_ref[...]
    off_out[0] = off_ref[...]

    for walker in range(OWN):
        tiles[0:1, walker * K:(walker + 1) * K] = tile_ref[walker:walker + 1, :]
    ids = tiles[0:1, 0:OWN * K]
    pick = (lax.broadcasted_iota(jnp.int32, (512, OWN * K), 0) == ids).astype(jnp.float32).astype(jnp.bfloat16)
    weights = wts_ref[...].reshape(OWN * K, 64).astype(jnp.float32).T
    load_table.wait()
    local = table.shape[1]
    total = jnp.zeros((local, OWN * K), jnp.float32)
    for chunk in range(0, 64, 8):
        block = table[chunk:chunk + 8].reshape(8 * local, 512)
        picked = jnp.dot(block, pick, preferred_element_type=jnp.float32)
        picked = picked.reshape(8, local, OWN * K)
        for c in range(8):
            total = total + picked[c] * weights[chunk + c:chunk + c + 1, :]
    change = total.T - old_ref[...].reshape(OWN * K, local)
    load_inv.wait()
    for walker in range(OWN):
        left = change[walker * K:(walker + 1) * K]
        for block in range(0, BLOCKS, 4):
            out = jnp.dot(
                left, inv_out[walker, :, block * 128:(block + 4) * 128],
                precision=HI, preferred_element_type=jnp.float32,
            )
            for b in range(4):
                term[walker * BLOCKS + block + b] = out[:, b * 128:(b + 1) * 128]

    pl.semaphore_wait(barrier, n)

    def scatter(step, carry):
        peer = shifted(me, step, n, 1)
        pltpu.make_async_remote_copy(
            src_ref=term.at[pl.ds(peer * share, share)],
            dst_ref=parts.at[step],
            send_sem=rs_send, recv_sem=rs_recv,
            device_id={"orb": peer}, device_id_type=MESH,
        ).start()
        return carry

    lax.fori_loop(1, n, scatter, 0)

    copies = [
        pltpu.make_async_remote_copy(
            src_ref=inv_out.at[pl.ds(first, OTHER)], dst_ref=inv_out.at[pl.ds(OWN, OTHER)],
            send_sem=inv_send, recv_sem=inv_recv, device_id=partner, device_id_type=MESH,
        )
    ]
    for index, (ref, out) in enumerate(((elec_ref, elec_out), (acc_ref, acc_out), (off_ref, off_out))):
        copies.append(
            pltpu.make_async_remote_copy(
                src_ref=ref, dst_ref=out.at[1],
                send_sem=int_send.at[index], recv_sem=int_recv.at[index],
                device_id=partner, device_id_type=MESH,
            )
        )
    for copy in copies:
        copy.start()

    rest = parts.at[pl.ds(1, n - 1)]
    pltpu.make_async_copy(rest, rest, rs_recv).wait()
    summed = term[pl.ds(me * share, share)] + jnp.sum(parts[1:n], axis=0)
    rows_out[pl.ds(me * share, share)] = summed

    def forward(source):
        walker = lax.div(source * share, BLOCKS) if share <= BLOCKS else None
        wanted = jnp.logical_and(walker >= first, walker < first + OTHER)

        @pl.when(wanted)
        def _():
            pltpu.make_async_remote_copy(
                src_ref=rows_out.at[pl.ds(source * share, share)],
                dst_ref=rows_out.at[pl.ds(OWN * BLOCKS + source * share - first * BLOCKS, share)],
                send_sem=fw_send, recv_sem=fw_recv,
                device_id=partner, device_id_type=MESH,
            ).start()

    def gather(step, carry):
        peer = shifted(me, step, n, 1)
        mine = rows_out.at[pl.ds(me * share, share)]
        pltpu.make_async_remote_copy(
            src_ref=mine, dst_ref=mine,
            send_sem=ag_send, recv_sem=ag_recv.at[step],
            device_id={"orb": peer}, device_id_type=MESH,
        ).start()
        return carry

    lax.fori_loop(1, n, gather, 0)
    forward(me)

    def arrive(step, carry):
        source = shifted(me, step, n, -1)
        slot = rows_out.at[pl.ds(source * share, share)]
        pltpu.make_async_copy(slot, slot, ag_recv.at[step]).wait()
        forward(source)
        return carry

    lax.fori_loop(1, n, arrive, 0)

    for copy in copies:
        copy.wait()
    pltpu.make_async_copy(rest, rest, rs_send).wait()
    pltpu.make_async_copy(rest, rest, ag_send).wait()
    moved = rows_out.at[pl.ds(OWN * BLOCKS, OTHER * BLOCKS)]
    pltpu.make_async_copy(moved, moved, fw_send).wait()
    pltpu.make_async_copy(moved, moved, fw_recv).wait()


def finish(rows_ref, inv_ref, elec_ref, acc_ref, off_ref, ratio_ref, out_ref, lanes):
    core = lax.axis_index("walk")
    local = inv_ref.shape[1]
    count = OWN + OTHER

    lanes[...] = jnp.zeros_like(lanes)
    for slot in range(count):
        for row, ref in enumerate((elec_ref, acc_ref)):
            if slot < OWN:
                value = ref[0, slot:slot + 1, :]
            else:
                value = ref[1, pl.ds(slot - OWN + core, 1), :]
            lanes[row:row + 1, slot * K:(slot + 1) * K] = value
    elec = lanes[0:1, :]
    lane = lax.broadcasted_iota(jnp.int32, (1, 128), 1)
    group, move = lane // K, lane % K
    spot = jnp.broadcast_to(elec % 128, (K, 128))
    home = elec // 128

    cross = jnp.zeros((K, 128), jnp.float32)
    left = jnp.zeros((local, 128), jnp.float32)
    wide = jnp.broadcast_to(elec % 128, (local, 128))
    for slot in range(count):
        for block in range(BLOCKS):
            hit = jnp.logical_and(group == slot, home == block)
            got = jnp.take_along_axis(rows_ref[slot * BLOCKS + block], spot, axis=1)
            cross = jnp.where(hit, got, cross)
            got = jnp.take_along_axis(inv_ref[slot, :, block * 128:(block + 1) * 128], wide, axis=1)
            left = jnp.where(hit, got, left)

    rowid = lax.broadcasted_iota(jnp.int32, (K, 128), 0)
    full = cross + jnp.where(rowid == move, 1.0, 0.0)
    cols = []
    accept = []
    accepts = jnp.broadcast_to(lanes[1:2, :], (K, 128))
    for j in range(K):
        index = jnp.broadcast_to(group * K + j, (K, 128))
        cols.append(jnp.take_along_axis(full, index, axis=1))
        accept.append(jnp.take_along_axis(accepts, index, axis=1) > 0)
    ratio = jnp.zeros((1, 128), jnp.float32)
    for n in range(K):
        pivot = cols[n][n:n + 1, :]
        ratio = jnp.where(move == n, pivot, ratio)
        scale = 1.0 / pivot
        column = cols[n]
        here = rowid == n
        for j in range(K):
            row = (scale if j == n else cols[j][n:n + 1, :] * scale)
            base = (jnp.zeros_like(column) if j == n else cols[j])
            value = jnp.where(here, row, base - column * row)
            cols[j] = jnp.where(accept[n], value, cols[j])
    small = jnp.zeros((K, 128), jnp.float32)
    for j in range(K):
        rowmask = jnp.zeros((K, 128), jnp.bool_)
        small = jnp.where(move == j, cols[j], small)
    taken_cols = accepts > 0
    taken_rows = jnp.zeros((K, 128), jnp.float32)
    for i in range(K):
        taken_rows = jnp.where(rowid == i, accept[i].astype(jnp.float32), taken_rows)
    small = jnp.where(jnp.logical_and(taken_cols, taken_rows > 0), small, 0.0)
    for walker in range(OWN):
        ratio_ref[walker:walker + 1, :] = ratio[:, walker * K:(walker + 1) * K]

    stacked = jnp.concatenate([small] * 8, axis=0)
    rowgroup = lax.broadcasted_iota(jnp.int32, (128, 128), 0) // K
    square = jnp.where(rowgroup == group, stacked, 0.0)
    mix = jnp.dot(left, square, precision=HI, preferred_element_type=jnp.float32)

    w8 = lax.broadcasted_iota(jnp.int32, (8, 128), 0)
    counts = jnp.zeros((8, 128), jnp.int32)
    lane8 = lax.broadcasted_iota(jnp.int32, (8, 128), 1)
    lanes[2:3, 0:OWN] = off_ref[0]
    lanes[3:4, 0:OWN] = off_ref[1]
    mine = lanes[2:3, :]
    theirs = lanes[3:4, :]
    low = jnp.where(core == 0, mine, theirs)
    high = jnp.where(core == 0, theirs, mine)
    first4 = jnp.where(jnp.logical_and(lane8 < OWN, lane8 <= w8), low, 0)
    last4 = jnp.where(jnp.logical_and(lane8 < OWN, lane8 + OWN <= w8), high, 0)
    ends = jnp.sum((first4 + last4).astype(jnp.float32), axis=1, keepdims=True)
    past = (ends <= (lane8 + OWN * core).astype(jnp.float32)).astype(jnp.float32)
    source = jnp.sum(past, axis=0, keepdims=True).astype(jnp.int32)
    local_id = source - OWN * core
    inside = jnp.logical_and(local_id >= 0, local_id < OWN)
    other = source - OWN * (1 - core) - (1 - core) * 0 - core
    slots = jnp.where(inside, local_id, OWN + jnp.clip(other, 0, OTHER - 1))

    picks = [slots[0, s] for s in range(OWN)]
    lhs = jnp.concatenate([jnp.where(group == picks[s], mix, 0.0) for s in range(OWN)], axis=0)
    lhs = lhs[:, :count * K]
    for block in range(0, BLOCKS, 2):
        rhs = jnp.concatenate(
            [
                jnp.concatenate([rows_ref[slot * BLOCKS + block + b] for slot in range(count)], axis=0)
                for b in range(2)
            ],
            axis=1,
        )
        product = jnp.dot(lhs, rhs, precision=HI, preferred_element_type=jnp.float32)
        columns = slice(block * 128, (block + 2) * 128)
        for s in range(OWN):
            out_ref[s, :, columns] = inv_ref[picks[s], :, columns] - product[s * local:(s + 1) * local]


def body(n, inverse, table, old_rows, spline_weights, tile_index, electrons, accepts, offspring):
    local = inverse.shape[1]
    share = OWN * BLOCKS // n
    vmem = pl.BlockSpec(memory_space=pltpu.VMEM)
    anywhere = pl.BlockSpec(memory_space=pl.ANY)
    f32, i32 = jnp.float32, jnp.int32
    rows, inv_all, elec_all, acc_all, off_all = pl.pallas_call(
        functools.partial(exchange, n),
        out_shape=(
            jax.ShapeDtypeStruct(((OWN + OTHER) * BLOCKS, K, 128), f32),
            jax.ShapeDtypeStruct((OWN + OTHER, local, 2048), f32),
            jax.ShapeDtypeStruct((2, OWN, K), i32),
            jax.ShapeDtypeStruct((2, OWN, K), i32),
            jax.ShapeDtypeStruct((2, 1, OWN), i32),
        ),
        in_specs=[anywhere, anywhere] + [vmem] * 6,
        out_specs=(vmem,) * 5,
        scratch_shapes=[
            pltpu.VMEM((64, local, 512), jnp.bfloat16),
            pltpu.VMEM((OWN * BLOCKS, K, 128), f32),
            pltpu.VMEM((n, share, K, 128), f32),
            pltpu.VMEM((8, 128), i32),
            pltpu.SemaphoreType.DMA((2,)),
            pltpu.SemaphoreType.DMA,
            pltpu.SemaphoreType.DMA,
            pltpu.SemaphoreType.DMA((3,)),
            pltpu.SemaphoreType.DMA((3,)),
            pltpu.SemaphoreType.DMA,
            pltpu.SemaphoreType.DMA,
            pltpu.SemaphoreType.DMA,
            pltpu.SemaphoreType.DMA((n,)),
            pltpu.SemaphoreType.DMA,
            pltpu.SemaphoreType.DMA,
        ],
        compiler_params=pltpu.CompilerParams(collective_id=0, has_side_effects=True),
        name="exchange",
    )(
        inverse, jnp.transpose(table, (1, 2, 0)), old_rows, spline_weights, tile_index,
        electrons, accepts, offspring.reshape(1, OWN),
    )
    ratios, new_inverse = pl.pallas_call(
        finish,
        out_shape=(
            jax.ShapeDtypeStruct((OWN, K), f32),
            jax.ShapeDtypeStruct((OWN, local, 2048), f32),
        ),
        in_specs=[vmem] * 5,
        out_specs=(vmem, vmem),
        scratch_shapes=[pltpu.VMEM((8, 128), i32)],
        name="finish",
    )(rows, inv_all, elec_all, acc_all, off_all)
    return ratios, new_inverse


def solution(mesh):
    in_specs = (
        P("walk", "orb", None),
        P(None, None, "orb"),
        P("walk", None, "orb"),
        P("walk", None, None),
        P("walk", None),
        P("walk", None),
        P("walk", None),
        P("walk"),
    )
    out_specs = (P("walk", None), P("walk", "orb", None))
    return jax.shard_map(
        functools.partial(body, mesh.shape["orb"]),
        mesh=mesh, in_specs=in_specs, out_specs=out_specs, check_vma=False,
    )
```

```python
import functools

import jax
import jax.numpy as jnp
from jax import lax
from jax.experimental import pallas as pl
from jax.experimental.pallas import tpu as pltpu
from jax.sharding import PartitionSpec as P

MESH = pl.DeviceIdType.MESH
HI = lax.Precision.HIGHEST
OWN = 4
OTHER = 3
K = 16
BLOCKS = 16


def each_peer(me, n, sign, visit):
    if n != 64:
        for step in range(1, n):
            visit(step, lax.rem(me + sign * step + n, n))
        return
    z, y, x = lax.div(me, 16), lax.rem(lax.div(me, 4), 4), lax.rem(me, 4)
    xs = [lax.rem(x + sign * move + 4, 4) for move in range(4)]
    for move in range(1, 4):
        visit(move, z * 16 + y * 4 + xs[move])

    def line(index, carry):
        high = lax.rem(z + sign * lax.div(index, 4) + 4, 4)
        low = lax.rem(y + sign * lax.rem(index, 4) + 4, 4)
        for move in range(4):
            visit(index * 4 + move, high * 16 + low * 4 + xs[move])
        return carry

    lax.fori_loop(1, 16, line, 0)


def exchange(
    n,
    inv_hbm, table_hbm, old_ref, wts_ref, tile_ref, elec_ref, acc_ref, off_ref,
    rows_out, inv_out, elec_out, acc_out, off_out,
    table, term, parts, tiles,
    load_sem, inv_send, inv_recv, int_send, int_recv,
    rs_send, rs_recv, ag_send, ag_recv, fw_send, fw_recv,
):
    me = lax.axis_index("orb")
    core = lax.axis_index("walk")
    partner = {"walk": 1 - core}
    share = OWN * BLOCKS // n
    first = 1 - core

    barrier = pltpu.get_barrier_semaphore()

    load_inv = pltpu.make_async_copy(inv_hbm, inv_out.at[pl.ds(0, OWN)], load_sem.at[0])
    load_table = pltpu.make_async_copy(table_hbm, table, load_sem.at[1])
    load_table.start()
    load_inv.start()

    pl.semaphore_signal(barrier, inc=1, device_id=partner, device_id_type=MESH)

    def greet(step, peer):
        pl.semaphore_signal(barrier, inc=1, device_id={"orb": peer}, device_id_type=MESH)

    each_peer(me, n, 1, greet)

    elec_out[0] = elec_ref[...]
    acc_out[0] = acc_ref[...]
    off_out[0] = off_ref[...]

    for walker in range(OWN):
        tiles[0:1, walker * K:(walker + 1) * K] = tile_ref[walker:walker + 1, :]
    ids = tiles[0:1, 0:OWN * K]
    pick = (lax.broadcasted_iota(jnp.int32, (512, OWN * K), 0) == ids).astype(jnp.float32).astype(jnp.bfloat16)
    weights = wts_ref[...].reshape(OWN * K, 64).astype(jnp.float32).T
    load_table.wait()
    local = table.shape[1]
    total = jnp.zeros((local, OWN * K), jnp.float32)
    for chunk in range(0, 64, 8):
        block = table[chunk:chunk + 8].reshape(8 * local, 512)
        picked = jnp.dot(block, pick, preferred_element_type=jnp.float32)
        picked = picked.reshape(8, local, OWN * K)
        for c in range(8):
            total = total + picked[c] * weights[chunk + c:chunk + c + 1, :]
    change = total.T - old_ref[...].reshape(OWN * K, local)
    load_inv.wait()
    for walker in range(OWN):
        left = change[walker * K:(walker + 1) * K]
        for block in range(0, BLOCKS, 4):
            out = jnp.dot(
                left, inv_out[walker, :, block * 128:(block + 4) * 128],
                precision=HI, preferred_element_type=jnp.float32,
            )
            for b in range(4):
                term[walker * BLOCKS + block + b] = out[:, b * 128:(b + 1) * 128]

    pl.semaphore_wait(barrier, n)

    def scatter(step, peer):
        pltpu.make_async_remote_copy(
            src_ref=term.at[pl.ds(peer * share, share)],
            dst_ref=parts.at[step],
            send_sem=rs_send, recv_sem=rs_recv,
            device_id={"orb": peer}, device_id_type=MESH,
        ).start()

    each_peer(me, n, 1, scatter)

    copies = [
        pltpu.make_async_remote_copy(
            src_ref=inv_out.at[pl.ds(first, OTHER)], dst_ref=inv_out.at[pl.ds(OWN, OTHER)],
            send_sem=inv_send, recv_sem=inv_recv, device_id=partner, device_id_type=MESH,
        )
    ]
    for index, (ref, out) in enumerate(((elec_ref, elec_out), (acc_ref, acc_out), (off_ref, off_out))):
        copies.append(
            pltpu.make_async_remote_copy(
                src_ref=ref, dst_ref=out.at[1],
                send_sem=int_send.at[index], recv_sem=int_recv.at[index],
                device_id=partner, device_id_type=MESH,
            )
        )
    for copy in copies:
        copy.start()

    rest = parts.at[pl.ds(1, n - 1)]
    pltpu.make_async_copy(rest, rest, rs_recv).wait()
    summed = term[pl.ds(me * share, share)] + jnp.sum(parts[1:n], axis=0)
    rows_out[pl.ds(me * share, share)] = summed

    def forward(source):
        walker = lax.div(source * share, BLOCKS) if share <= BLOCKS else None
        wanted = jnp.logical_and(walker >= first, walker < first + OTHER)

        @pl.when(wanted)
        def _():
            pltpu.make_async_remote_copy(
                src_ref=rows_out.at[pl.ds(source * share, share)],
                dst_ref=rows_out.at[pl.ds(OWN * BLOCKS + source * share - first * BLOCKS, share)],
                send_sem=fw_send, recv_sem=fw_recv,
                device_id=partner, device_id_type=MESH,
            ).start()

    def gather(step, peer):
        mine = rows_out.at[pl.ds(me * share, share)]
        pltpu.make_async_remote_copy(
            src_ref=mine, dst_ref=mine,
            send_sem=ag_send, recv_sem=ag_recv.at[step],
            device_id={"orb": peer}, device_id_type=MESH,
        ).start()

    each_peer(me, n, 1, gather)
    forward(me)

    def arrive(step, source):
        slot = rows_out.at[pl.ds(source * share, share)]
        pltpu.make_async_copy(slot, slot, ag_recv.at[step]).wait()
        forward(source)

    each_peer(me, n, -1, arrive)

    for copy in copies:
        copy.wait()
    pltpu.make_async_copy(rest, rest, rs_send).wait()
    pltpu.make_async_copy(rest, rest, ag_send).wait()
    moved = rows_out.at[pl.ds(OWN * BLOCKS, OTHER * BLOCKS)]
    pltpu.make_async_copy(moved, moved, fw_send).wait()
    pltpu.make_async_copy(moved, moved, fw_recv).wait()


def finish(rows_ref, inv_ref, elec_ref, acc_ref, off_ref, ratio_ref, out_hbm, lanes, out_ref, out_sem):
    core = lax.axis_index("walk")
    local = inv_ref.shape[1]
    count = OWN + OTHER

    lanes[...] = jnp.zeros_like(lanes)
    for slot in range(count):
        for row, ref in enumerate((elec_ref, acc_ref)):
            if slot < OWN:
                value = ref[0, slot:slot + 1, :]
            else:
                value = ref[1, pl.ds(slot - OWN + core, 1), :]
            lanes[row:row + 1, slot * K:(slot + 1) * K] = value
    elec = lanes[0:1, :]
    lane = lax.broadcasted_iota(jnp.int32, (1, 128), 1)
    group, move = lane // K, lane % K
    spot = jnp.broadcast_to(elec % 128, (K, 128))
    home = elec // 128

    cross = jnp.zeros((K, 128), jnp.float32)
    left = jnp.zeros((local, 128), jnp.float32)
    wide = jnp.broadcast_to(elec % 128, (local, 128))
    for slot in range(count):
        for block in range(BLOCKS):
            hit = jnp.logical_and(group == slot, home == block)
            got = jnp.take_along_axis(rows_ref[slot * BLOCKS + block], spot, axis=1)
            cross = jnp.where(hit, got, cross)
            got = jnp.take_along_axis(inv_ref[slot, :, block * 128:(block + 1) * 128], wide, axis=1)
            left = jnp.where(hit, got, left)

    rowid = lax.broadcasted_iota(jnp.int32, (K, 128), 0)
    full = cross + jnp.where(rowid == move, 1.0, 0.0)
    cols = []
    accept = []
    accepts = jnp.broadcast_to(lanes[1:2, :], (K, 128))
    for j in range(K):
        index = jnp.broadcast_to(group * K + j, (K, 128))
        cols.append(jnp.take_along_axis(full, index, axis=1))
        accept.append(jnp.take_along_axis(accepts, index, axis=1) > 0)
    ratio = jnp.zeros((1, 128), jnp.float32)
    for n in range(K):
        pivot = cols[n][n:n + 1, :]
        ratio = jnp.where(move == n, pivot, ratio)
        scale = 1.0 / pivot
        column = cols[n]
        here = rowid == n
        for j in range(K):
            row = (scale if j == n else cols[j][n:n + 1, :] * scale)
            base = (jnp.zeros_like(column) if j == n else cols[j])
            value = jnp.where(here, row, base - column * row)
            cols[j] = jnp.where(accept[n], value, cols[j])
    small = jnp.zeros((K, 128), jnp.float32)
    for j in range(K):
        rowmask = jnp.zeros((K, 128), jnp.bool_)
        small = jnp.where(move == j, cols[j], small)
    taken_cols = accepts > 0
    taken_rows = jnp.zeros((K, 128), jnp.float32)
    for i in range(K):
        taken_rows = jnp.where(rowid == i, accept[i].astype(jnp.float32), taken_rows)
    small = jnp.where(jnp.logical_and(taken_cols, taken_rows > 0), small, 0.0)
    for walker in range(OWN):
        ratio_ref[walker:walker + 1, :] = ratio[:, walker * K:(walker + 1) * K]

    stacked = jnp.concatenate([small] * 8, axis=0)
    rowgroup = lax.broadcasted_iota(jnp.int32, (128, 128), 0) // K
    square = jnp.where(rowgroup == group, stacked, 0.0)
    mix = jnp.dot(left, square, precision=HI, preferred_element_type=jnp.float32)

    w8 = lax.broadcasted_iota(jnp.int32, (8, 128), 0)
    counts = jnp.zeros((8, 128), jnp.int32)
    lane8 = lax.broadcasted_iota(jnp.int32, (8, 128), 1)
    lanes[2:3, 0:OWN] = off_ref[0]
    lanes[3:4, 0:OWN] = off_ref[1]
    mine = lanes[2:3, :]
    theirs = lanes[3:4, :]
    low = jnp.where(core == 0, mine, theirs)
    high = jnp.where(core == 0, theirs, mine)
    first4 = jnp.where(jnp.logical_and(lane8 < OWN, lane8 <= w8), low, 0)
    last4 = jnp.where(jnp.logical_and(lane8 < OWN, lane8 + OWN <= w8), high, 0)
    ends = jnp.sum((first4 + last4).astype(jnp.float32), axis=1, keepdims=True)
    past = (ends <= (lane8 + OWN * core).astype(jnp.float32)).astype(jnp.float32)
    source = jnp.sum(past, axis=0, keepdims=True).astype(jnp.int32)
    local_id = source - OWN * core
    inside = jnp.logical_and(local_id >= 0, local_id < OWN)
    other = source - OWN * (1 - core) - (1 - core) * 0 - core
    slots = jnp.where(inside, local_id, OWN + jnp.clip(other, 0, OTHER - 1))

    picks = [slots[0, s] for s in range(OWN)]
    lhs = jnp.concatenate([jnp.where(group == picks[s], mix, 0.0) for s in range(OWN)], axis=0)
    lhs = lhs[:, :count * K]
    for block in range(0, BLOCKS, 2):
        rhs = jnp.concatenate(
            [
                jnp.concatenate([rows_ref[slot * BLOCKS + block + b] for slot in range(count)], axis=0)
                for b in range(2)
            ],
            axis=1,
        )
        product = jnp.dot(lhs, rhs, precision=HI, preferred_element_type=jnp.float32)
        columns = slice(block * 128, (block + 2) * 128)
        for s in range(OWN):
            out_ref[s, :, columns] = inv_ref[picks[s], :, columns] - product[s * local:(s + 1) * local]
        if block % 4 == 2:
            done = pl.ds((block - 2) * 128, 512)
            pltpu.make_async_copy(out_ref.at[:, :, done], out_hbm.at[:, :, done], out_sem).start()
    pltpu.make_async_copy(out_ref, out_hbm, out_sem).wait()


def body(n, inverse, table, old_rows, spline_weights, tile_index, electrons, accepts, offspring):
    local = inverse.shape[1]
    share = OWN * BLOCKS // n
    vmem = pl.BlockSpec(memory_space=pltpu.VMEM)
    anywhere = pl.BlockSpec(memory_space=pl.ANY)
    f32, i32 = jnp.float32, jnp.int32
    rows, inv_all, elec_all, acc_all, off_all = pl.pallas_call(
        functools.partial(exchange, n),
        out_shape=(
            pltpu.VMEM(((OWN + OTHER) * BLOCKS, K, 128), f32),
            pltpu.VMEM((OWN + OTHER, local, 2048), f32),
            pltpu.VMEM((2, OWN, K), i32),
            pltpu.VMEM((2, OWN, K), i32),
            pltpu.VMEM((2, 1, OWN), i32),
        ),
        in_specs=[anywhere, anywhere] + [vmem] * 6,
        out_specs=(vmem,) * 5,
        scratch_shapes=[
            pltpu.VMEM((64, local, 512), jnp.bfloat16),
            pltpu.VMEM((OWN * BLOCKS, K, 128), f32),
            pltpu.VMEM((n, share, K, 128), f32),
            pltpu.VMEM((8, 128), i32),
            pltpu.SemaphoreType.DMA((2,)),
            pltpu.SemaphoreType.DMA,
            pltpu.SemaphoreType.DMA,
            pltpu.SemaphoreType.DMA((3,)),
            pltpu.SemaphoreType.DMA((3,)),
            pltpu.SemaphoreType.DMA,
            pltpu.SemaphoreType.DMA,
            pltpu.SemaphoreType.DMA,
            pltpu.SemaphoreType.DMA((n,)),
            pltpu.SemaphoreType.DMA,
            pltpu.SemaphoreType.DMA,
        ],
        compiler_params=pltpu.CompilerParams(collective_id=0, has_side_effects=True),
        name="exchange",
    )(
        inverse, jnp.transpose(table, (1, 2, 0)), old_rows, spline_weights, tile_index,
        electrons, accepts, offspring.reshape(1, OWN),
    )
    kept = [
        pltpu.with_memory_space_constraint(x, pltpu.VMEM)
        for x in (rows, inv_all, elec_all, acc_all, off_all)
    ]
    ratios, new_inverse = pl.pallas_call(
        finish,
        out_shape=(
            jax.ShapeDtypeStruct((OWN, K), f32),
            jax.ShapeDtypeStruct((OWN, local, 2048), f32),
        ),
        in_specs=[vmem] * 5,
        out_specs=(vmem, anywhere),
        scratch_shapes=[
            pltpu.VMEM((8, 128), i32),
            pltpu.VMEM((OWN, local, 2048), f32),
            pltpu.SemaphoreType.DMA,
        ],
        name="finish",
    )(*kept)
    return ratios, new_inverse


def solution(mesh):
    in_specs = (
        P("walk", "orb", None),
        P(None, None, "orb"),
        P("walk", None, "orb"),
        P("walk", None, None),
        P("walk", None),
        P("walk", None),
        P("walk", None),
        P("walk"),
    )
    out_specs = (P("walk", None), P("walk", "orb", None))
    return jax.shard_map(
        functools.partial(body, mesh.shape["orb"]),
        mesh=mesh, in_specs=in_specs, out_specs=out_specs, check_vma=False,
    )
```

```python
import functools

import jax
import jax.numpy as jnp
from jax import lax
from jax.experimental import pallas as pl
from jax.experimental.pallas import tpu as pltpu
from jax.sharding import PartitionSpec as P

MESH = pl.DeviceIdType.MESH
HI = lax.Precision.HIGHEST
OWN = 4
OTHER = 3
K = 16
BLOCKS = 16
PAIRS = 2
TILES = 64
WALK = 32


def halves(x):
    high = x.astype(jnp.bfloat16)
    return high, (x - high.astype(jnp.float32)).astype(jnp.bfloat16)


def each_peer(me, n, sign, visit):
    if n != 64:
        for step in range(1, n):
            visit(step, lax.rem(me + sign * step + n, n))
        return
    z, y, x = lax.div(me, 16), lax.rem(lax.div(me, 4), 4), lax.rem(me, 4)
    xs = [lax.rem(x + sign * move + 4, 4) for move in range(4)]
    for move in range(1, 4):
        visit(move, z * 16 + y * 4 + xs[move])

    def line(index, carry):
        high = lax.rem(z + sign * lax.div(index, 4) + 4, 4)
        low = lax.rem(y + sign * lax.rem(index, 4) + 4, 4)
        for move in range(4):
            visit(index * 4 + move, high * 16 + low * 4 + xs[move])
        return carry

    lax.fori_loop(1, 16, line, 0)


def exchange(
    n,
    inv_hbm, table_hbm, old_ref, wts_ref, tile_ref, elec_ref, acc_ref, off_ref,
    rows_out, inv_out, elec_out, acc_out, off_out,
    table, term, parts, tiles,
    load_sem, inv_send, inv_recv, int_send, int_recv,
    rs_send, rs_recv, ag_send, ag_recv, fw_send, fw_recv,
):
    me = lax.axis_index("orb")
    core = lax.axis_index("walk")
    partner = {"walk": 1 - core}
    share = TILES // n
    first = 1 - core

    barrier = pltpu.get_barrier_semaphore()

    load_inv = pltpu.make_async_copy(inv_hbm, inv_out.at[pl.ds(0, OWN)], load_sem.at[0])
    load_table = pltpu.make_async_copy(table_hbm, table, load_sem.at[1])
    load_table.start()
    load_inv.start()

    pl.semaphore_signal(barrier, inc=1, device_id=partner, device_id_type=MESH)

    def greet(step, peer):
        pl.semaphore_signal(barrier, inc=1, device_id={"orb": peer}, device_id_type=MESH)

    each_peer(me, n, 1, greet)

    elec_out[0] = elec_ref[...]
    acc_out[0] = acc_ref[...]
    off_out[0] = off_ref[...]

    for walker in range(OWN):
        tiles[0:1, walker * K:(walker + 1) * K] = tile_ref[walker:walker + 1, :]
    ids = tiles[0:1, 0:OWN * K]
    pick = (lax.broadcasted_iota(jnp.int32, (512, OWN * K), 0) == ids).astype(jnp.float32).astype(jnp.bfloat16)
    weights = wts_ref[...].reshape(OWN * K, 64).astype(jnp.float32).T
    load_table.wait()
    local = table.shape[1]
    total = jnp.zeros((local, OWN * K), jnp.float32)
    for chunk in range(0, 64, 8):
        block = table[chunk:chunk + 8].reshape(8 * local, 512)
        picked = jnp.dot(block, pick, preferred_element_type=jnp.float32)
        picked = picked.reshape(8, local, OWN * K)
        for c in range(8):
            total = total + picked[c] * weights[chunk + c:chunk + c + 1, :]
    change = total.T - old_ref[...].reshape(OWN * K, local)
    load_inv.wait()

    def project(pair):
        for index in range(2):
            walker = 2 * pair + index
            high, low = halves(change[walker * K:(walker + 1) * K])
            left = jnp.concatenate([high, high, low], axis=1)
            for block in range(0, BLOCKS, 4):
                high, low = halves(inv_out[walker, :, block * 128:(block + 4) * 128])
                right = jnp.concatenate([high, low, high], axis=0)
                out = jnp.dot(left, right, preferred_element_type=jnp.float32)
                for b in range(4):
                    for half in range(2):
                        tile = index * WALK + (block + b) * 2 + half
                        term[pair, tile] = out[half * 8:half * 8 + 8, b * 128:(b + 1) * 128]

    def scatter(pair):
        def visit(step, peer):
            pltpu.make_async_remote_copy(
                src_ref=term.at[pair, pl.ds(peer * share, share)],
                dst_ref=parts.at[pair, step],
                send_sem=rs_send.at[pair], recv_sem=rs_recv.at[pair],
                device_id={"orb": peer}, device_id_type=MESH,
            ).start()

        each_peer(me, n, 1, visit)

    project(0)
    pl.semaphore_wait(barrier, n)
    scatter(0)

    copies = [
        pltpu.make_async_remote_copy(
            src_ref=inv_out.at[pl.ds(first, OTHER)], dst_ref=inv_out.at[pl.ds(OWN, OTHER)],
            send_sem=inv_send, recv_sem=inv_recv, device_id=partner, device_id_type=MESH,
        )
    ]
    for index, (ref, out) in enumerate(((elec_ref, elec_out), (acc_ref, acc_out), (off_ref, off_out))):
        copies.append(
            pltpu.make_async_remote_copy(
                src_ref=ref, dst_ref=out.at[1],
                send_sem=int_send.at[index], recv_sem=int_recv.at[index],
                device_id=partner, device_id_type=MESH,
            )
        )
    for copy in copies:
        copy.start()

    project(1)
    scatter(1)

    def place(pair, owner):
        return pair * TILES + owner * share

    def forward(pair, owner):
        walker = 2 * pair + lax.div(owner * share, WALK)
        wanted = jnp.logical_and(walker >= first, walker < first + OTHER)

        @pl.when(wanted)
        def _():
            pltpu.make_async_remote_copy(
                src_ref=rows_out.at[pl.ds(place(pair, owner), share)],
                dst_ref=rows_out.at[pl.ds(OWN * WALK + place(pair, owner) - first * WALK, share)],
                send_sem=fw_send, recv_sem=fw_recv,
                device_id=partner, device_id_type=MESH,
            ).start()

    rest = [parts.at[pair, pl.ds(1, n - 1)] for pair in range(PAIRS)]
    for pair in range(PAIRS):
        pltpu.make_async_copy(rest[pair], rest[pair], rs_recv.at[pair]).wait()
        mine = pl.ds(me * share, share)
        rows_out[pl.ds(place(pair, me), share)] = term[pair, mine] + jnp.sum(parts[pair, 1:n], axis=0)

        def gather(step, peer):
            block = rows_out.at[pl.ds(place(pair, me), share)]
            pltpu.make_async_remote_copy(
                src_ref=block, dst_ref=block,
                send_sem=ag_send.at[pair], recv_sem=ag_recv.at[pair, step],
                device_id={"orb": peer}, device_id_type=MESH,
            ).start()

        each_peer(me, n, 1, gather)
        forward(pair, me)

    for pair in range(PAIRS):
        def arrive(step, owner):
            slot = rows_out.at[pl.ds(place(pair, owner), share)]
            pltpu.make_async_copy(slot, slot, ag_recv.at[pair, step]).wait()
            forward(pair, owner)

        each_peer(me, n, -1, arrive)

    for copy in copies:
        copy.wait()
    for pair in range(PAIRS):
        pltpu.make_async_copy(rest[pair], rest[pair], rs_send.at[pair]).wait()
        pltpu.make_async_copy(rest[pair], rest[pair], ag_send.at[pair]).wait()
    moved = rows_out.at[pl.ds(OWN * WALK, OTHER * WALK)]
    pltpu.make_async_copy(moved, moved, fw_send).wait()
    pltpu.make_async_copy(moved, moved, fw_recv).wait()


def finish(rows_ref, inv_ref, elec_ref, acc_ref, off_ref, ratio_ref, out_hbm, lanes, out_ref, out_sem):
    core = lax.axis_index("walk")
    local = inv_ref.shape[1]
    count = OWN + OTHER

    lanes[...] = jnp.zeros_like(lanes)
    for slot in range(count):
        for row, ref in enumerate((elec_ref, acc_ref)):
            if slot < OWN:
                value = ref[0, slot:slot + 1, :]
            else:
                value = ref[1, pl.ds(slot - OWN + core, 1), :]
            lanes[row:row + 1, slot * K:(slot + 1) * K] = value
    elec = lanes[0:1, :]
    lane = lax.broadcasted_iota(jnp.int32, (1, 128), 1)
    group, move = lane // K, lane % K
    spot = jnp.broadcast_to(elec % 128, (K, 128))
    home = elec // 128

    cross = jnp.zeros((K, 128), jnp.float32)
    left = jnp.zeros((local, 128), jnp.float32)
    wide = jnp.broadcast_to(elec % 128, (local, 128))
    for slot in range(count):
        for block in range(BLOCKS):
            hit = jnp.logical_and(group == slot, home == block)
            got = jnp.take_along_axis(
                rows_ref[pl.ds(slot * WALK + block * 2, 2)].reshape(K, 128), spot, axis=1
            )
            cross = jnp.where(hit, got, cross)
            got = jnp.take_along_axis(inv_ref[slot, :, block * 128:(block + 1) * 128], wide, axis=1)
            left = jnp.where(hit, got, left)

    rowid = lax.broadcasted_iota(jnp.int32, (K, 128), 0)
    full = cross + jnp.where(rowid == move, 1.0, 0.0)
    cols = []
    accept = []
    accepts = jnp.broadcast_to(lanes[1:2, :], (K, 128))
    for j in range(K):
        index = jnp.broadcast_to(group * K + j, (K, 128))
        cols.append(jnp.take_along_axis(full, index, axis=1))
        accept.append(jnp.take_along_axis(accepts, index, axis=1) > 0)
    ratio = jnp.zeros((1, 128), jnp.float32)
    for n in range(K):
        pivot = cols[n][n:n + 1, :]
        ratio = jnp.where(move == n, pivot, ratio)
        scale = 1.0 / pivot
        column = cols[n]
        here = rowid == n
        for j in range(K):
            row = (scale if j == n else cols[j][n:n + 1, :] * scale)
            base = (jnp.zeros_like(column) if j == n else cols[j])
            value = jnp.where(here, row, base - column * row)
            cols[j] = jnp.where(accept[n], value, cols[j])
    small = jnp.zeros((K, 128), jnp.float32)
    for j in range(K):
        rowmask = jnp.zeros((K, 128), jnp.bool_)
        small = jnp.where(move == j, cols[j], small)
    taken_cols = accepts > 0
    taken_rows = jnp.zeros((K, 128), jnp.float32)
    for i in range(K):
        taken_rows = jnp.where(rowid == i, accept[i].astype(jnp.float32), taken_rows)
    small = jnp.where(jnp.logical_and(taken_cols, taken_rows > 0), small, 0.0)
    for walker in range(OWN):
        ratio_ref[walker:walker + 1, :] = ratio[:, walker * K:(walker + 1) * K]

    w8 = lax.broadcasted_iota(jnp.int32, (8, 128), 0)
    counts = jnp.zeros((8, 128), jnp.int32)
    lane8 = lax.broadcasted_iota(jnp.int32, (8, 128), 1)
    lanes[2:3, 0:OWN] = off_ref[0]
    lanes[3:4, 0:OWN] = off_ref[1]
    mine = lanes[2:3, :]
    theirs = lanes[3:4, :]
    low = jnp.where(core == 0, mine, theirs)
    high = jnp.where(core == 0, theirs, mine)
    first4 = jnp.where(jnp.logical_and(lane8 < OWN, lane8 <= w8), low, 0)
    last4 = jnp.where(jnp.logical_and(lane8 < OWN, lane8 + OWN <= w8), high, 0)
    ends = jnp.sum((first4 + last4).astype(jnp.float32), axis=1, keepdims=True)
    past = (ends <= (lane8 + OWN * core).astype(jnp.float32)).astype(jnp.float32)
    source = jnp.sum(past, axis=0, keepdims=True).astype(jnp.int32)
    local_id = source - OWN * core
    inside = jnp.logical_and(local_id >= 0, local_id < OWN)
    other = source - OWN * (1 - core) - (1 - core) * 0 - core
    slots = jnp.where(inside, local_id, OWN + jnp.clip(other, 0, OTHER - 1))

    picks = [slots[0, s] for s in range(OWN)]
    stacked = jnp.concatenate([small] * 8, axis=0)
    rows128 = lax.broadcasted_iota(jnp.int32, (128, 128), 0)
    square = jnp.where(rows128 // K == group, stacked, 0.0)
    repeat = jnp.where(rows128 % K == move, 1.0, 0.0)
    square = jnp.dot(square, repeat, precision=HI, preferred_element_type=jnp.float32)
    chosen = jnp.concatenate([jnp.where(group == picks[s], left, 0.0) for s in range(OWN)], axis=0)
    mix = jnp.dot(chosen, square, precision=HI, preferred_element_type=jnp.float32)
    target = lax.broadcasted_iota(jnp.int32, (OWN * local, 128), 0) // local
    whole = jnp.where(group % OWN == target, mix, 0.0)
    high, low = halves(whole)
    lhs = jnp.concatenate([high, low], axis=1)[:, :3 * OWN * K]
    for block in range(0, BLOCKS, 2):
        high, low = halves(
            jnp.concatenate(
                [
                    jnp.concatenate(
                        [
                            rows_ref[pl.ds(picks[s] * WALK + (block + b) * 2, 2)].reshape(K, 128)
                            for s in range(OWN)
                        ],
                        axis=0,
                    )
                    for b in range(2)
                ],
                axis=1,
            )
        )
        rhs = jnp.concatenate([high, low, high], axis=0)
        product = jnp.dot(lhs, rhs, preferred_element_type=jnp.float32)
        columns = slice(block * 128, (block + 2) * 128)
        for s in range(OWN):
            out_ref[s, :, columns] = inv_ref[picks[s], :, columns] - product[s * local:(s + 1) * local]
        if block % 4 == 2:
            done = pl.ds((block - 2) * 128, 512)
            pltpu.make_async_copy(out_ref.at[:, :, done], out_hbm.at[:, :, done], out_sem).start()
    pltpu.make_async_copy(out_ref, out_hbm, out_sem).wait()


def body(n, inverse, table, old_rows, spline_weights, tile_index, electrons, accepts, offspring):
    local = inverse.shape[1]
    share = TILES // n
    vmem = pl.BlockSpec(memory_space=pltpu.VMEM)
    anywhere = pl.BlockSpec(memory_space=pl.ANY)
    f32, i32 = jnp.float32, jnp.int32
    rows, inv_all, elec_all, acc_all, off_all = pl.pallas_call(
        functools.partial(exchange, n),
        out_shape=(
            pltpu.VMEM(((OWN + OTHER) * WALK, 8, 128), f32),
            pltpu.VMEM((OWN + OTHER, local, 2048), f32),
            pltpu.VMEM((2, OWN, K), i32),
            pltpu.VMEM((2, OWN, K), i32),
            pltpu.VMEM((2, 1, OWN), i32),
        ),
        in_specs=[anywhere, anywhere] + [vmem] * 6,
        out_specs=(vmem,) * 5,
        scratch_shapes=[
            pltpu.VMEM((64, local, 512), jnp.bfloat16),
            pltpu.VMEM((PAIRS, TILES, 8, 128), f32),
            pltpu.VMEM((PAIRS, n, share, 8, 128), f32),
            pltpu.VMEM((8, 128), i32),
            pltpu.SemaphoreType.DMA((2,)),
            pltpu.SemaphoreType.DMA,
            pltpu.SemaphoreType.DMA,
            pltpu.SemaphoreType.DMA((3,)),
            pltpu.SemaphoreType.DMA((3,)),
            pltpu.SemaphoreType.DMA((PAIRS,)),
            pltpu.SemaphoreType.DMA((PAIRS,)),
            pltpu.SemaphoreType.DMA((PAIRS,)),
            pltpu.SemaphoreType.DMA((PAIRS, n)),
            pltpu.SemaphoreType.DMA,
            pltpu.SemaphoreType.DMA,
        ],
        compiler_params=pltpu.CompilerParams(collective_id=0, has_side_effects=True),
        name="exchange",
    )(
        inverse, jnp.transpose(table, (1, 2, 0)), old_rows, spline_weights, tile_index,
        electrons, accepts, offspring.reshape(1, OWN),
    )
    kept = [
        pltpu.with_memory_space_constraint(x, pltpu.VMEM)
        for x in (rows, inv_all, elec_all, acc_all, off_all)
    ]
    ratios, new_inverse = pl.pallas_call(
        finish,
        out_shape=(
            jax.ShapeDtypeStruct((OWN, K), f32),
            jax.ShapeDtypeStruct((OWN, local, 2048), f32),
        ),
        in_specs=[vmem] * 5,
        out_specs=(vmem, anywhere),
        scratch_shapes=[
            pltpu.VMEM((8, 128), i32),
            pltpu.VMEM((OWN, local, 2048), f32),
            pltpu.SemaphoreType.DMA,
        ],
        name="finish",
    )(*kept)
    return ratios, new_inverse


def solution(mesh):
    in_specs = (
        P("walk", "orb", None),
        P(None, None, "orb"),
        P("walk", None, "orb"),
        P("walk", None, None),
        P("walk", None),
        P("walk", None),
        P("walk", None),
        P("walk"),
    )
    out_specs = (P("walk", None), P("walk", "orb", None))
    return jax.shard_map(
        functools.partial(body, mesh.shape["orb"]),
        mesh=mesh, in_specs=in_specs, out_specs=out_specs, check_vma=False,
    )
```

```python
import functools

import jax
import jax.numpy as jnp
from jax import lax
from jax.experimental import pallas as pl
from jax.experimental.pallas import tpu as pltpu
from jax.sharding import PartitionSpec as P

MESH = pl.DeviceIdType.MESH
HI = lax.Precision.HIGHEST
OWN = 4
OTHER = 3
K = 16
BLOCKS = 16
PAIRS = 1
TILES = 128 // PAIRS
WALK = 32


def halves(x):
    high = x.astype(jnp.bfloat16)
    return high, (x - high.astype(jnp.float32)).astype(jnp.bfloat16)


def each_peer(me, n, sign, visit, far=False):
    if n != 64:
        for step in range(1, n):
            visit(step, lax.rem(me + sign * step + n, n))
        return
    z, y, x = lax.div(me, 16), lax.rem(lax.div(me, 4), 4), lax.rem(me, 4)
    moves = (2, 3, 1, 0) if far else (0, 1, 3, 2)
    xs = {move: lax.rem(x + sign * move + 4, 4) for move in moves}

    def own():
        for move in moves:
            if move:
                visit(move, z * 16 + y * 4 + xs[move])

    def line(index, carry):
        index = 15 - index if far else index
        high, low = lax.div(index, 4), lax.rem(index, 4)
        high = high + lax.div(high, 2) * (5 - 2 * high)
        low = low + lax.div(low, 2) * (5 - 2 * low)
        base = 16 * lax.rem(z + sign * high + 4, 4) + 4 * lax.rem(y + sign * low + 4, 4)
        for move in moves:
            visit(high * 16 + low * 4 + move, base + xs[move])
        return carry

    if far:
        lax.fori_loop(0, 15, line, 0)
        own()
    else:
        own()
        lax.fori_loop(1, 16, line, 0)


def exchange(
    n,
    inv_hbm, table_hbm, old_ref, wts_ref, tile_ref, elec_ref, acc_ref, off_ref,
    rows_out, inv_out, lanes, left_out,
    elec_out, acc_out, off_out, table, term, parts, tiles,
    load_sem, inv_send, inv_recv, int_send, int_recv,
    rs_send, rs_recv, ag_send, ag_recv, fw_send, fw_recv,
):
    me = lax.axis_index("orb")
    core = lax.axis_index("walk")
    partner = {"walk": 1 - core}
    share = TILES // n
    first = 1 - core

    barrier = pltpu.get_barrier_semaphore()

    load_inv = pltpu.make_async_copy(inv_hbm, inv_out.at[pl.ds(0, OWN)], load_sem.at[4])
    load_table = [
        pltpu.make_async_copy(table_hbm.at[pl.ds(16 * c, 16)], table.at[pl.ds(16 * c, 16)], load_sem.at[c])
        for c in range(4)
    ]
    for load in load_table:
        load.start()
    load_inv.start()

    pl.semaphore_signal(barrier, inc=1, device_id=partner, device_id_type=MESH)

    def greet(step, peer):
        pl.semaphore_signal(barrier, inc=1, device_id={"orb": peer}, device_id_type=MESH)

    each_peer(me, n, 1, greet, True)

    elec_out[0] = elec_ref[...]
    acc_out[0] = acc_ref[...]
    off_out[0] = off_ref[...]

    for walker in range(OWN):
        tiles[0:1, walker * K:(walker + 1) * K] = tile_ref[walker:walker + 1, :]
    ids = tiles[0:1, 0:OWN * K]
    pick = (lax.broadcasted_iota(jnp.int32, (512, OWN * K), 0) == ids).astype(jnp.float32).astype(jnp.bfloat16)
    weights = wts_ref[...].reshape(OWN * K, 64).astype(jnp.float32).T
    local = table.shape[1]
    total = jnp.zeros((local, OWN * K), jnp.float32)
    for chunk in range(0, 64, 8):
        if chunk % 16 == 0:
            load_table[chunk // 16].wait()
        block = table[chunk:chunk + 8].reshape(8 * local, 512)
        picked = jnp.dot(block, pick, preferred_element_type=jnp.float32)
        picked = picked.reshape(8, local, OWN * K)
        for c in range(8):
            total = total + picked[c] * weights[chunk + c:chunk + c + 1, :]
    change = total.T - old_ref[...].reshape(OWN * K, local)
    load_inv.wait()

    def project(pair):
        for index in range(OWN // PAIRS):
            walker = OWN // PAIRS * pair + index
            high, low = halves(change[walker * K:(walker + 1) * K])
            left = jnp.concatenate([high, high, low], axis=1)
            for block in range(0, BLOCKS, 4):
                high, low = halves(inv_out[walker, :, block * 128:(block + 4) * 128])
                right = jnp.concatenate([high, low, high], axis=0)
                out = jnp.dot(left, right, preferred_element_type=jnp.float32)
                for b in range(4):
                    for half in range(2):
                        tile = index * WALK + (block + b) * 2 + half
                        term[pair, tile] = out[half * 8:half * 8 + 8, b * 128:(b + 1) * 128]

    def scatter(pair):
        def visit(step, peer):
            pltpu.make_async_remote_copy(
                src_ref=term.at[pair, pl.ds(peer * share, share)],
                dst_ref=parts.at[pair, step],
                send_sem=rs_send.at[pair], recv_sem=rs_recv.at[pair],
                device_id={"orb": peer}, device_id_type=MESH,
            ).start()

        each_peer(me, n, 1, visit, True)

    project(0)
    pl.semaphore_wait(barrier, n)
    scatter(0)

    copies = [
        pltpu.make_async_remote_copy(
            src_ref=inv_out.at[pl.ds(first, OTHER)], dst_ref=inv_out.at[pl.ds(OWN, OTHER)],
            send_sem=inv_send, recv_sem=inv_recv, device_id=partner, device_id_type=MESH,
        )
    ]
    for index, (ref, out) in enumerate(((elec_ref, elec_out), (acc_ref, acc_out), (off_ref, off_out))):
        copies.append(
            pltpu.make_async_remote_copy(
                src_ref=ref, dst_ref=out.at[1],
                send_sem=int_send.at[index], recv_sem=int_recv.at[index],
                device_id=partner, device_id_type=MESH,
            )
        )
    for copy in copies:
        copy.start()

    for pair in range(1, PAIRS):
        project(pair)
        scatter(pair)

    def place(pair, owner):
        return pair * TILES + owner * share

    def forward(pair, owner):
        walker = OWN // PAIRS * pair + lax.div(owner * share, WALK)
        wanted = jnp.logical_and(walker >= first, walker < first + OTHER)

        @pl.when(wanted)
        def _():
            pltpu.make_async_remote_copy(
                src_ref=rows_out.at[pl.ds(place(pair, owner), share)],
                dst_ref=rows_out.at[pl.ds(OWN * WALK + place(pair, owner) - first * WALK, share)],
                send_sem=fw_send, recv_sem=fw_recv,
                device_id=partner, device_id_type=MESH,
            ).start()

    rest = [parts.at[pair, pl.ds(1, n - 1)] for pair in range(PAIRS)]
    for pair in range(PAIRS):
        pltpu.make_async_copy(rest[pair], rest[pair], rs_recv.at[pair]).wait()
        mine = pl.ds(me * share, share)
        rows_out[pl.ds(place(pair, me), share)] = term[pair, mine] + jnp.sum(parts[pair, 1:n], axis=0)

        def gather(step, peer):
            block = rows_out.at[pl.ds(place(pair, me), share)]
            pltpu.make_async_remote_copy(
                src_ref=block, dst_ref=block,
                send_sem=ag_send.at[pair], recv_sem=ag_recv.at[pair, step],
                device_id={"orb": peer}, device_id_type=MESH,
            ).start()

        each_peer(me, n, 1, gather, True)
        forward(pair, me)

    for copy in copies:
        copy.wait()

    lanes[...] = jnp.zeros_like(lanes)
    for slot in range(OWN + OTHER):
        for row, ref in enumerate((elec_out, acc_out)):
            if slot < OWN:
                value = ref[0, slot:slot + 1, :]
            else:
                value = ref[1, pl.ds(slot - OWN + core, 1), :]
            lanes[row:row + 1, slot * K:(slot + 1) * K] = value
    for row in range(2):
        lanes[2 + row:3 + row, 0:OWN] = off_out[row]

    elec = lanes[0:1, :]
    lane = lax.broadcasted_iota(jnp.int32, (1, 128), 1)
    wide = jnp.broadcast_to(elec % 128, (local, 128))
    columns = jnp.zeros((local, 128), jnp.float32)
    for slot in range(OWN + OTHER):
        for block in range(BLOCKS):
            hit = jnp.logical_and(lane // K == slot, elec // 128 == block)
            got = jnp.take_along_axis(inv_out[slot, :, block * 128:(block + 1) * 128], wide, axis=1)
            columns = jnp.where(hit, got, columns)
    left_out[...] = columns

    for pair in range(PAIRS):
        def arrive(step, owner):
            slot = rows_out.at[pl.ds(place(pair, owner), share)]
            pltpu.make_async_copy(slot, slot, ag_recv.at[pair, step]).wait()
            forward(pair, owner)

        each_peer(me, n, -1, arrive)

    for pair in range(PAIRS):
        pltpu.make_async_copy(rest[pair], rest[pair], rs_send.at[pair]).wait()
        pltpu.make_async_copy(rest[pair], rest[pair], ag_send.at[pair]).wait()
    moved = rows_out.at[pl.ds(OWN * WALK, OTHER * WALK)]
    pltpu.make_async_copy(moved, moved, fw_send).wait()
    pltpu.make_async_copy(moved, moved, fw_recv).wait()


def finish(rows_ref, inv_ref, lanes, left_ref, ratio_ref, out_hbm, out_ref, out_sem):
    core = lax.axis_index("walk")
    local = inv_ref.shape[1]
    count = OWN + OTHER

    elec = lanes[0:1, :]
    lane = lax.broadcasted_iota(jnp.int32, (1, 128), 1)
    group, move = lane // K, lane % K
    spot = jnp.broadcast_to(elec % 128, (K, 128))
    home = elec // 128

    left = left_ref[...]
    cross = jnp.zeros((K, 128), jnp.float32)
    for slot in range(count):
        for block in range(BLOCKS):
            hit = jnp.logical_and(group == slot, home == block)
            got = jnp.take_along_axis(
                rows_ref[pl.ds(slot * WALK + block * 2, 2)].reshape(K, 128), spot, axis=1
            )
            cross = jnp.where(hit, got, cross)

    rowid = lax.broadcasted_iota(jnp.int32, (K, 128), 0)
    full = cross + jnp.where(rowid == move, 1.0, 0.0)
    cols = []
    accept = []
    accepts = jnp.broadcast_to(lanes[1:2, :], (K, 128))
    for j in range(K):
        index = jnp.broadcast_to(group * K + j, (K, 128))
        cols.append(jnp.take_along_axis(full, index, axis=1))
        accept.append(jnp.take_along_axis(accepts, index, axis=1) > 0)
    ratio = jnp.zeros((1, 128), jnp.float32)
    for n in range(K):
        pivot = cols[n][n:n + 1, :]
        ratio = jnp.where(move == n, pivot, ratio)
        scale = 1.0 / pivot
        column = cols[n]
        here = rowid == n
        for j in range(K):
            row = (scale if j == n else cols[j][n:n + 1, :] * scale)
            base = (jnp.zeros_like(column) if j == n else cols[j])
            value = jnp.where(here, row, base - column * row)
            cols[j] = jnp.where(accept[n], value, cols[j])
    small = jnp.zeros((K, 128), jnp.float32)
    for j in range(K):
        rowmask = jnp.zeros((K, 128), jnp.bool_)
        small = jnp.where(move == j, cols[j], small)
    taken_cols = accepts > 0
    taken_rows = jnp.zeros((K, 128), jnp.float32)
    for i in range(K):
        taken_rows = jnp.where(rowid == i, accept[i].astype(jnp.float32), taken_rows)
    small = jnp.where(jnp.logical_and(taken_cols, taken_rows > 0), small, 0.0)
    for walker in range(OWN):
        ratio_ref[walker:walker + 1, :] = ratio[:, walker * K:(walker + 1) * K]

    w8 = lax.broadcasted_iota(jnp.int32, (8, 128), 0)
    counts = jnp.zeros((8, 128), jnp.int32)
    lane8 = lax.broadcasted_iota(jnp.int32, (8, 128), 1)
    mine = lanes[2:3, :]
    theirs = lanes[3:4, :]
    low = jnp.where(core == 0, mine, theirs)
    high = jnp.where(core == 0, theirs, mine)
    first4 = jnp.where(jnp.logical_and(lane8 < OWN, lane8 <= w8), low, 0)
    last4 = jnp.where(jnp.logical_and(lane8 < OWN, lane8 + OWN <= w8), high, 0)
    ends = jnp.sum((first4 + last4).astype(jnp.float32), axis=1, keepdims=True)
    past = (ends <= (lane8 + OWN * core).astype(jnp.float32)).astype(jnp.float32)
    source = jnp.sum(past, axis=0, keepdims=True).astype(jnp.int32)
    local_id = source - OWN * core
    inside = jnp.logical_and(local_id >= 0, local_id < OWN)
    other = source - OWN * (1 - core) - (1 - core) * 0 - core
    slots = jnp.where(inside, local_id, OWN + jnp.clip(other, 0, OTHER - 1))

    picks = [slots[0, s] for s in range(OWN)]
    stacked = jnp.concatenate([small] * 8, axis=0)
    rows128 = lax.broadcasted_iota(jnp.int32, (128, 128), 0)
    square = jnp.where(rows128 // K == group, stacked, 0.0)
    repeat = jnp.where(rows128 % K == move, 1.0, 0.0)
    square = jnp.dot(square, repeat, precision=HI, preferred_element_type=jnp.float32)
    chosen = jnp.concatenate([jnp.where(group == picks[s], left, 0.0) for s in range(OWN)], axis=0)
    mix = jnp.dot(chosen, square, precision=HI, preferred_element_type=jnp.float32)
    target = lax.broadcasted_iota(jnp.int32, (OWN * local, 128), 0) // local
    whole = jnp.where(group % OWN == target, mix, 0.0)
    high, low = halves(whole)
    lhs = jnp.concatenate([high, low], axis=1)[:, :3 * OWN * K]
    for block in range(0, BLOCKS, 2):
        high, low = halves(
            jnp.concatenate(
                [
                    jnp.concatenate(
                        [
                            rows_ref[pl.ds(picks[s] * WALK + (block + b) * 2, 2)].reshape(K, 128)
                            for s in range(OWN)
                        ],
                        axis=0,
                    )
                    for b in range(2)
                ],
                axis=1,
            )
        )
        rhs = jnp.concatenate([high, low, high], axis=0)
        product = jnp.dot(lhs, rhs, preferred_element_type=jnp.float32)
        columns = slice(block * 128, (block + 2) * 128)
        for s in range(OWN):
            out_ref[s, :, columns] = inv_ref[picks[s], :, columns] - product[s * local:(s + 1) * local]
        if block % 4 == 2:
            done = pl.ds((block - 2) * 128, 512)
            pltpu.make_async_copy(out_ref.at[:, :, done], out_hbm.at[:, :, done], out_sem).start()
    pltpu.make_async_copy(out_ref, out_hbm, out_sem).wait()


def body(n, inverse, table, old_rows, spline_weights, tile_index, electrons, accepts, offspring):
    local = inverse.shape[1]
    share = TILES // n
    vmem = pl.BlockSpec(memory_space=pltpu.VMEM)
    anywhere = pl.BlockSpec(memory_space=pl.ANY)
    f32, i32 = jnp.float32, jnp.int32
    kept = pl.pallas_call(
        functools.partial(exchange, n),
        out_shape=(
            pltpu.VMEM(((OWN + OTHER) * WALK, 8, 128), f32),
            pltpu.VMEM((OWN + OTHER, local, 2048), f32),
            pltpu.VMEM((8, 128), i32),
            pltpu.VMEM((local, 128), f32),
        ),
        in_specs=[anywhere, anywhere] + [vmem] * 6,
        out_specs=(vmem,) * 4,
        scratch_shapes=[
            pltpu.VMEM((2, OWN, K), i32),
            pltpu.VMEM((2, OWN, K), i32),
            pltpu.VMEM((2, 1, OWN), i32),
            pltpu.VMEM((64, local, 512), jnp.bfloat16),
            pltpu.VMEM((PAIRS, TILES, 8, 128), f32),
            pltpu.VMEM((PAIRS, n, share, 8, 128), f32),
            pltpu.VMEM((8, 128), i32),
            pltpu.SemaphoreType.DMA((5,)),
            pltpu.SemaphoreType.DMA,
            pltpu.SemaphoreType.DMA,
            pltpu.SemaphoreType.DMA((3,)),
            pltpu.SemaphoreType.DMA((3,)),
            pltpu.SemaphoreType.DMA((PAIRS,)),
            pltpu.SemaphoreType.DMA((PAIRS,)),
            pltpu.SemaphoreType.DMA((PAIRS,)),
            pltpu.SemaphoreType.DMA((PAIRS, n)),
            pltpu.SemaphoreType.DMA,
            pltpu.SemaphoreType.DMA,
        ],
        compiler_params=pltpu.CompilerParams(collective_id=0, has_side_effects=True),
        name="exchange",
    )(
        inverse, jnp.transpose(table, (1, 2, 0)), old_rows, spline_weights, tile_index,
        electrons, accepts, offspring.reshape(1, OWN),
    )
    kept = [
        pltpu.with_memory_space_constraint(x, pltpu.VMEM)
        for x in kept
    ]
    ratios, new_inverse = pl.pallas_call(
        finish,
        out_shape=(
            jax.ShapeDtypeStruct((OWN, K), f32),
            jax.ShapeDtypeStruct((OWN, local, 2048), f32),
        ),
        in_specs=[vmem] * 4,
        out_specs=(vmem, anywhere),
        scratch_shapes=[
            pltpu.VMEM((OWN, local, 2048), f32),
            pltpu.SemaphoreType.DMA,
        ],
        name="finish",
    )(*kept)
    return ratios, new_inverse


def solution(mesh):
    in_specs = (
        P("walk", "orb", None),
        P(None, None, "orb"),
        P("walk", None, "orb"),
        P("walk", None, None),
        P("walk", None),
        P("walk", None),
        P("walk", None),
        P("walk"),
    )
    out_specs = (P("walk", None), P("walk", "orb", None))
    return jax.shard_map(
        functools.partial(body, mesh.shape["orb"]),
        mesh=mesh, in_specs=in_specs, out_specs=out_specs, check_vma=False,
    )
```

```python
import functools

import jax
import jax.numpy as jnp
from jax import lax
from jax.experimental import pallas as pl
from jax.experimental.pallas import tpu as pltpu
from jax.sharding import PartitionSpec as P

MESH = pl.DeviceIdType.MESH
HI = lax.Precision.HIGHEST
OWN = 4
OTHER = 3
K = 16
BLOCKS = 16
PAIRS = 1
TILES = 128 // PAIRS
WALK = 32


def halves(x):
    high = x.astype(jnp.bfloat16)
    return high, (x - high.astype(jnp.float32)).astype(jnp.bfloat16)


def hops(step):
    return sum(min(d, 4 - d) for d in (step // 16, step // 4 % 4, step % 4))


def diagonal(i, m):
    return (i // 4 + m) % 4 * 16 + (i % 4 + m) % 4 * 4 + m


MIXED = [diagonal(i, m) for i in range(16) for m in range(4) if i or m]
FAR = sorted(MIXED, key=lambda step: -hops(step))


def each_peer(me, n, sign, visit, order=FAR):
    if n != 64:
        for step in range(1, n):
            visit(step, lax.rem(me + sign * step + n, n))
        return
    digits = [
        [scale * lax.rem(lax.rem(lax.div(me, scale), 4) + sign * move + 4, 4) for move in range(4)]
        for scale in (16, 4, 1)
    ]
    for step in order:
        visit(step, digits[0][step // 16] + digits[1][step // 4 % 4] + digits[2][step % 4])


def exchange(
    n,
    inv_hbm, table_hbm, old_ref, wts_ref, tile_ref, elec_ref, acc_ref, off_ref,
    rows_out, inv_out, lanes, left_out,
    elec_out, acc_out, off_out, table, term, parts, tiles,
    load_sem, inv_send, inv_recv, int_send, int_recv,
    rs_send, rs_recv, ag_send, ag_recv, fw_send, fw_recv,
):
    me = lax.axis_index("orb")
    core = lax.axis_index("walk")
    partner = {"walk": 1 - core}
    share = TILES // n
    first = 1 - core

    barrier = pltpu.get_barrier_semaphore()

    load_inv = pltpu.make_async_copy(inv_hbm, inv_out.at[pl.ds(0, OWN)], load_sem.at[4])
    load_table = [
        pltpu.make_async_copy(table_hbm.at[pl.ds(16 * c, 16)], table.at[pl.ds(16 * c, 16)], load_sem.at[c])
        for c in range(4)
    ]
    for load in load_table:
        load.start()
    load_inv.start()

    pl.semaphore_signal(barrier, inc=1, device_id=partner, device_id_type=MESH)

    def greet(step, peer):
        pl.semaphore_signal(barrier, inc=1, device_id={"orb": peer}, device_id_type=MESH)

    each_peer(me, n, 1, greet)

    elec_out[0] = elec_ref[...]
    acc_out[0] = acc_ref[...]
    off_out[0] = off_ref[...]

    for walker in range(OWN):
        tiles[0:1, walker * K:(walker + 1) * K] = tile_ref[walker:walker + 1, :]
    ids = tiles[0:1, 0:OWN * K]
    pick = (lax.broadcasted_iota(jnp.int32, (512, OWN * K), 0) == ids).astype(jnp.float32).astype(jnp.bfloat16)
    weights = wts_ref[...].reshape(OWN * K, 64).astype(jnp.float32).T
    local = table.shape[1]
    total = jnp.zeros((local, OWN * K), jnp.float32)
    for chunk in range(0, 64, 8):
        if chunk % 16 == 0:
            load_table[chunk // 16].wait()
        block = table[chunk:chunk + 8].reshape(8 * local, 512)
        picked = jnp.dot(block, pick, preferred_element_type=jnp.float32)
        picked = picked.reshape(8, local, OWN * K)
        for c in range(8):
            total = total + picked[c] * weights[chunk + c:chunk + c + 1, :]
    change = total.T - old_ref[...].reshape(OWN * K, local)
    load_inv.wait()

    def project(pair):
        for index in range(OWN // PAIRS):
            walker = OWN // PAIRS * pair + index
            high, low = halves(change[walker * K:(walker + 1) * K])
            left = jnp.concatenate([high, high, low], axis=1)
            for block in range(0, BLOCKS, 4):
                high, low = halves(inv_out[walker, :, block * 128:(block + 4) * 128])
                right = jnp.concatenate([high, low, high], axis=0)
                out = jnp.dot(left, right, preferred_element_type=jnp.float32)
                for b in range(4):
                    for half in range(2):
                        tile = index * WALK + (block + b) * 2 + half
                        term[pair, tile] = out[half * 8:half * 8 + 8, b * 128:(b + 1) * 128]

    def scatter(pair):
        def visit(step, peer):
            pltpu.make_async_remote_copy(
                src_ref=term.at[pair, pl.ds(peer * share, share)],
                dst_ref=parts.at[pair, step],
                send_sem=rs_send.at[pair], recv_sem=rs_recv.at[pair],
                device_id={"orb": peer}, device_id_type=MESH,
            ).start()

        each_peer(me, n, 1, visit)

    project(0)
    pl.semaphore_wait(barrier, n)
    scatter(0)

    copies = [
        pltpu.make_async_remote_copy(
            src_ref=inv_out.at[pl.ds(first, OTHER)], dst_ref=inv_out.at[pl.ds(OWN, OTHER)],
            send_sem=inv_send, recv_sem=inv_recv, device_id=partner, device_id_type=MESH,
        )
    ]
    for index, (ref, out) in enumerate(((elec_ref, elec_out), (acc_ref, acc_out), (off_ref, off_out))):
        copies.append(
            pltpu.make_async_remote_copy(
                src_ref=ref, dst_ref=out.at[1],
                send_sem=int_send.at[index], recv_sem=int_recv.at[index],
                device_id=partner, device_id_type=MESH,
            )
        )
    for copy in copies:
        copy.start()

    for pair in range(1, PAIRS):
        project(pair)
        scatter(pair)

    def place(pair, owner):
        return pair * TILES + owner * share

    def forward(pair, owner):
        walker = OWN // PAIRS * pair + lax.div(owner * share, WALK)
        wanted = jnp.logical_and(walker >= first, walker < first + OTHER)

        @pl.when(wanted)
        def _():
            pltpu.make_async_remote_copy(
                src_ref=rows_out.at[pl.ds(place(pair, owner), share)],
                dst_ref=rows_out.at[pl.ds(OWN * WALK + place(pair, owner) - first * WALK, share)],
                send_sem=fw_send, recv_sem=fw_recv,
                device_id=partner, device_id_type=MESH,
            ).start()

    rest = [parts.at[pair, pl.ds(1, n - 1)] for pair in range(PAIRS)]
    for pair in range(PAIRS):
        pltpu.make_async_copy(rest[pair], rest[pair], rs_recv.at[pair]).wait()
        mine = pl.ds(me * share, share)
        rows_out[pl.ds(place(pair, me), share)] = term[pair, mine] + jnp.sum(parts[pair, 1:n], axis=0)

        def gather(step, peer):
            block = rows_out.at[pl.ds(place(pair, me), share)]
            pltpu.make_async_remote_copy(
                src_ref=block, dst_ref=block,
                send_sem=ag_send.at[pair], recv_sem=ag_recv.at[pair, step],
                device_id={"orb": peer}, device_id_type=MESH,
            ).start()

        each_peer(me, n, 1, gather)
        forward(pair, me)

    for copy in copies:
        copy.wait()

    lanes[...] = jnp.zeros_like(lanes)
    for slot in range(OWN + OTHER):
        for row, ref in enumerate((elec_out, acc_out)):
            if slot < OWN:
                value = ref[0, slot:slot + 1, :]
            else:
                value = ref[1, pl.ds(slot - OWN + core, 1), :]
            lanes[row:row + 1, slot * K:(slot + 1) * K] = value
    for row in range(2):
        lanes[2 + row:3 + row, 0:OWN] = off_out[row]

    elec = lanes[0:1, :]
    lane = lax.broadcasted_iota(jnp.int32, (1, 128), 1)
    wide = jnp.broadcast_to(elec % 128, (local, 128))
    columns = jnp.zeros((local, 128), jnp.float32)
    for slot in range(OWN + OTHER):
        for block in range(BLOCKS):
            hit = jnp.logical_and(lane // K == slot, elec // 128 == block)
            got = jnp.take_along_axis(inv_out[slot, :, block * 128:(block + 1) * 128], wide, axis=1)
            columns = jnp.where(hit, got, columns)
    left_out[...] = columns

    for pair in range(PAIRS):
        def arrive(step, owner):
            slot = rows_out.at[pl.ds(place(pair, owner), share)]
            pltpu.make_async_copy(slot, slot, ag_recv.at[pair, step]).wait()
            forward(pair, owner)

        each_peer(me, n, -1, arrive)

    for pair in range(PAIRS):
        pltpu.make_async_copy(rest[pair], rest[pair], rs_send.at[pair]).wait()
        pltpu.make_async_copy(rest[pair], rest[pair], ag_send.at[pair]).wait()
    moved = rows_out.at[pl.ds(OWN * WALK, OTHER * WALK)]
    pltpu.make_async_copy(moved, moved, fw_send).wait()
    pltpu.make_async_copy(moved, moved, fw_recv).wait()


def finish(rows_ref, inv_ref, lanes, left_ref, ratio_ref, out_hbm, out_ref, out_sem):
    core = lax.axis_index("walk")
    local = inv_ref.shape[1]
    count = OWN + OTHER

    elec = lanes[0:1, :]
    lane = lax.broadcasted_iota(jnp.int32, (1, 128), 1)
    group, move = lane // K, lane % K
    spot = jnp.broadcast_to(elec % 128, (K, 128))
    home = elec // 128

    left = left_ref[...]
    cross = jnp.zeros((K, 128), jnp.float32)
    for slot in range(count):
        for block in range(BLOCKS):
            hit = jnp.logical_and(group == slot, home == block)
            got = jnp.take_along_axis(
                rows_ref[pl.ds(slot * WALK + block * 2, 2)].reshape(K, 128), spot, axis=1
            )
            cross = jnp.where(hit, got, cross)

    rowid = lax.broadcasted_iota(jnp.int32, (K, 128), 0)
    full = cross + jnp.where(rowid == move, 1.0, 0.0)
    cols = []
    accept = []
    accepts = jnp.broadcast_to(lanes[1:2, :], (K, 128))
    for j in range(K):
        index = jnp.broadcast_to(group * K + j, (K, 128))
        cols.append(jnp.take_along_axis(full, index, axis=1))
        accept.append(jnp.take_along_axis(accepts, index, axis=1) > 0)
    ratio = jnp.zeros((1, 128), jnp.float32)
    for n in range(K):
        pivot = cols[n][n:n + 1, :]
        ratio = jnp.where(move == n, pivot, ratio)
        scale = 1.0 / pivot
        column = cols[n]
        here = rowid == n
        for j in range(K):
            row = (scale if j == n else cols[j][n:n + 1, :] * scale)
            base = (jnp.zeros_like(column) if j == n else cols[j])
            value = jnp.where(here, row, base - column * row)
            cols[j] = jnp.where(accept[n], value, cols[j])
    small = jnp.zeros((K, 128), jnp.float32)
    for j in range(K):
        rowmask = jnp.zeros((K, 128), jnp.bool_)
        small = jnp.where(move == j, cols[j], small)
    taken_cols = accepts > 0
    taken_rows = jnp.zeros((K, 128), jnp.float32)
    for i in range(K):
        taken_rows = jnp.where(rowid == i, accept[i].astype(jnp.float32), taken_rows)
    small = jnp.where(jnp.logical_and(taken_cols, taken_rows > 0), small, 0.0)
    for walker in range(OWN):
        ratio_ref[walker:walker + 1, :] = ratio[:, walker * K:(walker + 1) * K]

    w8 = lax.broadcasted_iota(jnp.int32, (8, 128), 0)
    counts = jnp.zeros((8, 128), jnp.int32)
    lane8 = lax.broadcasted_iota(jnp.int32, (8, 128), 1)
    mine = lanes[2:3, :]
    theirs = lanes[3:4, :]
    low = jnp.where(core == 0, mine, theirs)
    high = jnp.where(core == 0, theirs, mine)
    first4 = jnp.where(jnp.logical_and(lane8 < OWN, lane8 <= w8), low, 0)
    last4 = jnp.where(jnp.logical_and(lane8 < OWN, lane8 + OWN <= w8), high, 0)
    ends = jnp.sum((first4 + last4).astype(jnp.float32), axis=1, keepdims=True)
    past = (ends <= (lane8 + OWN * core).astype(jnp.float32)).astype(jnp.float32)
    source = jnp.sum(past, axis=0, keepdims=True).astype(jnp.int32)
    local_id = source - OWN * core
    inside = jnp.logical_and(local_id >= 0, local_id < OWN)
    other = source - OWN * (1 - core) - (1 - core) * 0 - core
    slots = jnp.where(inside, local_id, OWN + jnp.clip(other, 0, OTHER - 1))

    picks = [slots[0, s] for s in range(OWN)]
    stacked = jnp.concatenate([small] * 8, axis=0)
    rows128 = lax.broadcasted_iota(jnp.int32, (128, 128), 0)
    square = jnp.where(rows128 // K == group, stacked, 0.0)
    repeat = jnp.where(rows128 % K == move, 1.0, 0.0)
    square = jnp.dot(square, repeat, precision=HI, preferred_element_type=jnp.float32)
    chosen = jnp.concatenate([jnp.where(group == picks[s], left, 0.0) for s in range(OWN)], axis=0)
    mix = jnp.dot(chosen, square, precision=HI, preferred_element_type=jnp.float32)
    target = lax.broadcasted_iota(jnp.int32, (OWN * local, 128), 0) // local
    whole = jnp.where(group % OWN == target, mix, 0.0)
    high, low = halves(whole)
    lhs = jnp.concatenate([high, low], axis=1)[:, :3 * OWN * K]
    for block in range(0, BLOCKS, 2):
        high, low = halves(
            jnp.concatenate(
                [
                    jnp.concatenate(
                        [
                            rows_ref[pl.ds(picks[s] * WALK + (block + b) * 2, 2)].reshape(K, 128)
                            for s in range(OWN)
                        ],
                        axis=0,
                    )
                    for b in range(2)
                ],
                axis=1,
            )
        )
        rhs = jnp.concatenate([high, low, high], axis=0)
        product = jnp.dot(lhs, rhs, preferred_element_type=jnp.float32)
        columns = slice(block * 128, (block + 2) * 128)
        for s in range(OWN):
            out_ref[s, :, columns] = inv_ref[picks[s], :, columns] - product[s * local:(s + 1) * local]
        if block % 4 == 2:
            done = pl.ds((block - 2) * 128, 512)
            pltpu.make_async_copy(out_ref.at[:, :, done], out_hbm.at[:, :, done], out_sem).start()
    pltpu.make_async_copy(out_ref, out_hbm, out_sem).wait()


def body(n, inverse, table, old_rows, spline_weights, tile_index, electrons, accepts, offspring):
    local = inverse.shape[1]
    share = TILES // n
    vmem = pl.BlockSpec(memory_space=pltpu.VMEM)
    anywhere = pl.BlockSpec(memory_space=pl.ANY)
    f32, i32 = jnp.float32, jnp.int32
    kept = pl.pallas_call(
        functools.partial(exchange, n),
        out_shape=(
            pltpu.VMEM(((OWN + OTHER) * WALK, 8, 128), f32),
            pltpu.VMEM((OWN + OTHER, local, 2048), f32),
            pltpu.VMEM((8, 128), i32),
            pltpu.VMEM((local, 128), f32),
        ),
        in_specs=[anywhere, anywhere] + [vmem] * 6,
        out_specs=(vmem,) * 4,
        scratch_shapes=[
            pltpu.VMEM((2, OWN, K), i32),
            pltpu.VMEM((2, OWN, K), i32),
            pltpu.VMEM((2, 1, OWN), i32),
            pltpu.VMEM((64, local, 512), jnp.bfloat16),
            pltpu.VMEM((PAIRS, TILES, 8, 128), f32),
            pltpu.VMEM((PAIRS, n, share, 8, 128), f32),
            pltpu.VMEM((8, 128), i32),
            pltpu.SemaphoreType.DMA((5,)),
            pltpu.SemaphoreType.DMA,
            pltpu.SemaphoreType.DMA,
            pltpu.SemaphoreType.DMA((3,)),
            pltpu.SemaphoreType.DMA((3,)),
            pltpu.SemaphoreType.DMA((PAIRS,)),
            pltpu.SemaphoreType.DMA((PAIRS,)),
            pltpu.SemaphoreType.DMA((PAIRS,)),
            pltpu.SemaphoreType.DMA((PAIRS, n)),
            pltpu.SemaphoreType.DMA,
            pltpu.SemaphoreType.DMA,
        ],
        compiler_params=pltpu.CompilerParams(collective_id=0, has_side_effects=True),
        name="exchange",
    )(
        inverse, jnp.transpose(table, (1, 2, 0)), old_rows, spline_weights, tile_index,
        electrons, accepts, offspring.reshape(1, OWN),
    )
    kept = [
        pltpu.with_memory_space_constraint(x, pltpu.VMEM)
        for x in kept
    ]
    ratios, new_inverse = pl.pallas_call(
        finish,
        out_shape=(
            jax.ShapeDtypeStruct((OWN, K), f32),
            jax.ShapeDtypeStruct((OWN, local, 2048), f32),
        ),
        in_specs=[vmem] * 4,
        out_specs=(vmem, anywhere),
        scratch_shapes=[
            pltpu.VMEM((OWN, local, 2048), f32),
            pltpu.SemaphoreType.DMA,
        ],
        name="finish",
    )(*kept)
    return ratios, new_inverse


def solution(mesh):
    in_specs = (
        P("walk", "orb", None),
        P(None, None, "orb"),
        P("walk", None, "orb"),
        P("walk", None, None),
        P("walk", None),
        P("walk", None),
        P("walk", None),
        P("walk"),
    )
    out_specs = (P("walk", None), P("walk", "orb", None))
    return jax.shard_map(
        functools.partial(body, mesh.shape["orb"]),
        mesh=mesh, in_specs=in_specs, out_specs=out_specs, check_vma=False,
    )
```
